256 devices in a mesh: region: 8 (over y_hi, x), blk: 32 (over z, y_lo, core).
Axes of the slice: x: 4, y: 4 (y_hi: 2, y_lo: 2; y = y_hi * 2 + y_lo), z: 8, core: 2. Of those that a mesh axis runs over, the one named last changes fastest.
Arguments:
- probes: bfloat16 [2, 16, 131072], P(None, None, ('region', 'blk')), may hold values from -6 to 6
- near_blocks: bfloat16 [3, 2, 131072, 512], P(None, None, ('region', 'blk')), may hold values from -0.078125 to 0.078125
- inner_basis: bfloat16 [2, 64, 131072], P(None, None, ('region', 'blk')), may hold values from -0.1875 to 0.1875
- coupling: bfloat16 [2, 16384, 2048], P(None, ('region', 'blk')), may hold values from -0.09375 to 0.09375
- inner_expand: bfloat16 [2, 64, 131072], P(None, None, ('region', 'blk')), may hold values from -0.25 to 0.25
- outer_basis: bfloat16 [2, 256, 131072], P(None, None, ('region', 'blk')), may hold values from -0.1875 to 0.1875
- group_coupling: bfloat16 [2, 2048, 2048], P(None, 'region'), may hold values from -0.015625 to 0.015625
- outer_expand: bfloat16 [2, 256, 131072], P(None, None, ('region', 'blk')), may hold values from -0.125 to 0.125
- ranks: int32 [256], P(('region', 'blk')), may hold values from 8 to 64, as said below
Outputs:
- first: float32 [2, 16, 131072], P(None, None, ('region', 'blk'))
- second: float32 [2, 16, 131072], P(None, None, ('region', 'blk'))
The draws below stay inside these ranges and needn't reach their ends.
Inputs may be any that keep to these rules, and one draw needn't show every extreme that they name: `ranks`: some cluster has rank 64.
All inputs are finite; a program needn't handle non-finite values.
Results may differ from the reference program's by a relative error of at most 0.004.
Values may be sent and summed in bfloat16 or wider, within the bound.
No kernel may reach another device: no remote copies, remote signals or barrier semaphores. Data moves between devices by JAX's collectives and lax.ppermute only.
A program may use at most 64 MiB of HBM per device.

```python
import jax
import jax.numpy as jnp
from jax import lax

NL = 512
P_SIZE = 16
R = 64
RG = 256
NTOT = 131072
N_REGION = 8
N_BLK = 32
DEVICES = 256


def draw_ranks(key, part):
    first_key, second_key = jax.random.split(jax.random.fold_in(key, 11))
    values = jax.random.randint(first_key, (DEVICES,), R // 8, R + 1)
    chosen = jax.random.randint(second_key, (), 0, DEVICES)
    return jnp.where(jnp.arange(DEVICES) == chosen, R, values).astype(jnp.int32)


def block_levels(key, shape, cuts, smallest, high):
    loudness, own = 1.0, jax.random.fold_in(key, 6)
    for dim, blocks in cuts:
        heights = jnp.exp(jax.random.uniform(jax.random.fold_in(own, dim), (blocks,), jnp.float32, smallest / len(cuts), high / len(cuts)))
        loudness = loudness * jnp.repeat(heights, shape[dim] // blocks).reshape([-1 if axis == dim else 1 for axis in range(len(shape))])
    return loudness


def centred(key, shape, width, limit, pieces=(), held_as=jnp.bfloat16):
    entries = jax.random.normal(key, shape, jnp.float32) * width
    if len(pieces) > 0:
        entries = block_levels(key, shape, pieces, -0.22, 0.18) * entries
    return jnp.clip(entries, min=-limit, max=limit).astype(held_as)


def setup_inputs(seed: int = 0) -> dict:
    key_of = jax.random.split(jax.random.key(seed), 10)
    return {
        "probes": centred(key_of[0], (2, P_SIZE, NTOT), 1.0, 6.0, ((2, 256),)),
        "near_blocks": centred(key_of[1], (3, 2, NTOT, NL), (10 * NL) ** -0.5, 0.078125, ((2, 256),)),
        "inner_basis": centred(key_of[2], (2, R, NTOT), (2 * NL) ** -0.5, 0.1875, ((2, 256),)),
        "coupling": centred(key_of[3], (2, R * DEVICES, N_BLK * R), (2 * R * N_BLK) ** -0.5, 0.09375, ((1, 256),)),
        "inner_expand": centred(key_of[4], (2, R, NTOT), (10 * R) ** -0.5, 0.25, ((2, 256),)),
        "outer_basis": centred(key_of[5], (2, RG, NTOT), (2 * NL) ** -0.5, 0.1875, ((2, 256),)),
        "group_coupling": centred(key_of[6], (2, N_REGION * RG, N_REGION * RG), (2 * RG * N_REGION * N_BLK) ** -0.5, 0.015625, ((1, 8),)),
        "outer_expand": centred(key_of[7], (2, RG, NTOT), (10 * RG) ** -0.5, 0.125, ((2, 256),)),
        "ranks": draw_ranks(jax.random.fold_in(key_of[9], 71), 0),
    }


def dots(vec, mat):
    return jnp.dot(vec, mat.T, preferred_element_type=jnp.float32)


def cmul(mat, vec):
    real = dots(vec[0], mat[0]) - dots(vec[1], mat[1])
    imag = dots(vec[1], mat[0]) + dots(vec[0], mat[1])
    return jnp.stack([real, imag])


def cexpand(vec, mat):
    real = jnp.dot(vec[0], mat[0], preferred_element_type=jnp.float32) - jnp.dot(vec[1], mat[1], preferred_element_type=jnp.float32)
    imag = jnp.dot(vec[1], mat[0], preferred_element_type=jnp.float32) + jnp.dot(vec[0], mat[1], preferred_element_type=jnp.float32)
    return jnp.stack([real, imag])


def cmul_high(mat, vec):
    high = lax.Precision.HIGHEST
    real = jnp.dot(vec[0], mat[0].T, precision=high) - jnp.dot(vec[1], mat[1].T, precision=high)
    imag = jnp.dot(vec[1], mat[0].T, precision=high) + jnp.dot(vec[0], mat[1].T, precision=high)
    return jnp.stack([real, imag])


def per_device(arr, rows):
    count = N_REGION * N_BLK
    return jnp.moveaxis(arr.reshape(arr.shape[0], rows, count, arr.shape[-1] // count), 2, 0)


def apply_operator(vec, near_blocks, inner_basis, coupling, inner_expand, outer_basis, group_coupling, outer_expand, ranks):
    count = N_REGION * N_BLK
    spans = jnp.moveaxis(vec.reshape(2, P_SIZE, count, NL), 2, 0)
    grouped = spans.reshape(N_REGION, N_BLK, 2, P_SIZE, NL)
    blank = jnp.zeros_like(grouped[:, :1])
    before = jnp.concatenate([blank, grouped[:, :-1]], 1).reshape(count, 2, P_SIZE, NL)
    after = jnp.concatenate([grouped[:, 1:], blank], 1).reshape(count, 2, P_SIZE, NL)
    near_dev = jnp.moveaxis(near_blocks.reshape(3, 2, count, NL, NL), 2, 0)
    inner_dev = per_device(inner_basis, R)
    outer_dev = per_device(outer_basis, RG)

    def local(item):
        blocks, left, centre, right, basis_in, basis_out = item
        near = cmul(blocks[0], left) + cmul(blocks[1], centre) + cmul(blocks[2], right)
        return near, cmul(basis_in, centre), cmul(basis_out, centre)

    near, coeff, wide = lax.map(local, (near_dev, before, spans, after, inner_dev, outer_dev))
    keep = jnp.arange(R, dtype=jnp.int32)[None, :] < ranks[:, None]
    coeff = jnp.where(keep[:, None, None, :], coeff, jnp.zeros_like(coeff)).astype(jnp.bfloat16)
    cgroups = coeff.reshape(N_REGION, N_BLK, 2, P_SIZE, R)
    coupling_dev = jnp.moveaxis(coupling.reshape(2, count, R, N_BLK * R), 1, 0)

    def inner_term(item):
        rows, index = item
        grp = lax.dynamic_index_in_dim(cgroups, index // N_BLK, 0, keepdims=False)
        distant = jnp.abs(jnp.arange(N_BLK, dtype=jnp.int32) - index % N_BLK) > 1
        grp = jnp.where(distant[:, None, None, None], grp, jnp.zeros_like(grp))
        stacked = jnp.transpose(grp, (1, 2, 0, 3)).reshape(2, P_SIZE, N_BLK * R)
        return cmul(rows, stacked).astype(jnp.bfloat16)

    inner = lax.map(inner_term, (coupling_dev, jnp.arange(count, dtype=jnp.int32)))
    gsum = jnp.sum(wide.reshape(N_REGION, N_BLK, 2, P_SIZE, RG), axis=1)
    gmats = jnp.moveaxis(group_coupling.reshape(2, N_REGION, RG, N_REGION * RG), 1, 0)

    def outer_term(item):
        rows, index = item
        others = jnp.arange(N_REGION, dtype=jnp.int32) != index
        masked = jnp.where(others[:, None, None, None], gsum, jnp.zeros_like(gsum))
        stacked = jnp.transpose(masked, (1, 2, 0, 3)).reshape(2, P_SIZE, N_REGION * RG)
        return cmul_high(rows.astype(gsum.dtype), stacked).astype(jnp.bfloat16)

    field = lax.map(outer_term, (gmats, jnp.arange(N_REGION, dtype=jnp.int32)))
    field_dev = jnp.repeat(field, N_BLK, axis=0)
    expand_in = per_device(inner_expand, R)
    expand_out = per_device(outer_expand, RG)

    def finish(item):
        near_part, inner_part, field_part, basis_in, basis_out = item
        return near_part + cexpand(inner_part, basis_in) + cexpand(field_part, basis_out)

    result = lax.map(finish, (near, inner, field_dev, expand_in, expand_out))
    return jnp.moveaxis(result, 0, 2).reshape(2, P_SIZE, count * NL)


def reference(probes, near_blocks, inner_basis, coupling, inner_expand, outer_basis, group_coupling, outer_expand, ranks):
    args = (near_blocks, inner_basis, coupling, inner_expand, outer_basis, group_coupling, outer_expand, ranks)
    first = apply_operator(probes, *args)
    second = apply_operator(first.astype(jnp.bfloat16), *args)
    return first, second
```

```python
import functools

import jax
import jax.numpy as jnp
from jax import lax
from jax.experimental import pallas as pl
from jax.experimental.pallas import tpu as pltpu
from jax.sharding import Mesh
from jax.sharding import PartitionSpec as P

REGION = ("yh", "x")
BLK = ("z", "yl", "c")
PLANE = ("yh", "x", "yl", "c")
ALL = REGION + BLK
NT = (((1,), (1,)), ((), ()))
f32 = jnp.float32
bf16 = jnp.bfloat16


def vmem(n):
    return [pl.BlockSpec(memory_space=pltpu.VMEM)] * n


def nt(rows, mat):
    return lax.dot_general(rows, mat, NT, preferred_element_type=f32)


def nn(rows, mat):
    return jnp.dot(rows, mat, preferred_element_type=f32)


def halves(acc, width):
    real = acc[:16, :width] - acc[16:, width:]
    imag = acc[:16, width:] + acc[16:, :width]
    return real, imag


def paired(acc):
    lane = lax.broadcasted_iota(jnp.int32, (16, 128), 1)
    crossed = pltpu.roll(acc[16:], 64, 1)
    return acc[:16] + jnp.where(lane < 64, -crossed, crossed)


def fill_sends(vec, ranks, inner_basis, outer_basis, send):
    coeff = paired(nt(vec, inner_basis[...].reshape(128, 512)))
    lane = lax.broadcasted_iota(jnp.int32, (16, 128), 1)
    rank = jnp.where(lane < 64, lane, lane - 64)
    coeff = jnp.where(rank < ranks[0], coeff, 0.0).astype(bf16)
    real, imag = halves(nt(vec, outer_basis[...].reshape(512, 512)), 256)
    quarters = (real[:, :128], real[:, 128:], imag[:, :128], imag[:, 128:])
    quarters = [q.astype(bf16) for q in quarters]
    for d in range(32):
        send[d, :16] = coeff
        send[d, 16:] = quarters[d % 4]


def start_kernel(probes, ranks, inner_basis, outer_basis, send):
    fill_sends(probes[...].reshape(32, 512), ranks, inner_basis, outer_basis, send)


def sum_kernel(recv, send):
    total = recv[0, 16:].astype(f32)
    for j in range(1, 32):
        total = total + recv[j, 16:].astype(f32)
    total = total.astype(bf16)
    for d in range(32):
        send[d] = total


def local_kernel(index, before, vec, after, near_blocks, recv, coupling, inner_expand, out):
    acc = None
    for b, part in enumerate((before, vec, after)):
        term = nt(part[...].reshape(32, 512), near_blocks[b].reshape(1024, 512))
        acc = term if acc is None else acc + term
    real, imag = halves(acc, 512)
    lane = lax.broadcasted_iota(jnp.int32, (16, 128), 1)
    position = index[0]
    res, ims = [], []
    for j in range(0, 32, 2):
        first, second = (
            jnp.where(jnp.abs(k - position) > 1, recv[k, :16].astype(f32), 0.0) for k in (j, j + 1)
        )
        res.append(jnp.where(lane < 64, first, pltpu.roll(second, 64, 1)))
        ims.append(jnp.where(lane < 64, pltpu.roll(first, 64, 1), second))
    rows = jnp.concatenate([jnp.concatenate(res, 1), jnp.concatenate(ims, 1)], 0).astype(bf16)
    inner = paired(nt(rows, coupling[...].reshape(128, 2048)))
    rows = jnp.concatenate([inner[:, :64], pltpu.roll(inner, 64, 1)[:, :64]], 0).astype(bf16)
    a, b = nn(rows, inner_expand[0]), nn(rows, inner_expand[1])
    out[0] = real + (a[:16] - b[16:])
    out[1] = imag + (a[16:] + b[:16])


def field_part(index, recv, coupling, expand):
    region = index[1]
    res, ims = [], []
    for s in range(8):
        tiles = [jnp.where(s != region, recv[4 * s + q], jnp.zeros((16, 128), bf16)) for q in range(4)]
        res += tiles[:2]
        ims += tiles[2:]
    rows = jnp.concatenate([jnp.concatenate(res, 1), jnp.concatenate(ims, 1)], 0)
    real, imag = halves(nt(rows, coupling[...].reshape(512, 2048)), 256)
    rows = jnp.concatenate([real, imag], 0).astype(bf16)
    a, b = nn(rows, expand[0]), nn(rows, expand[1])
    return a[:16] - b[16:], a[16:] + b[:16]


def middle_kernel(index, recv, coupling, expand, local, ranks, inner_basis, outer_basis, first, vec, send):
    real, imag = field_part(index, recv, coupling, expand)
    real, imag = local[0] + real, local[1] + imag
    first[0] = real
    first[1] = imag
    rows = jnp.concatenate([real, imag], 0).astype(bf16)
    vec[0] = rows[:16]
    vec[1] = rows[16:]
    fill_sends(rows, ranks, inner_basis, outer_basis, send)


def last_kernel(index, recv, coupling, expand, local, second):
    real, imag = field_part(index, recv, coupling, expand)
    second[0] = local[0] + real
    second[1] = local[1] + imag


def shape(dims, dtype):
    return jax.ShapeDtypeStruct(dims, dtype)


SMEM = pl.BlockSpec(memory_space=pltpu.SMEM)
UP = [(i, i + 1) for i in range(31)]
DOWN = [(i + 1, i) for i in range(31)]


def exchange(value, axes):
    return lax.all_to_all(value, axes, split_axis=0, concat_axis=0, tiled=True)


def local_terms(index, vec, near_blocks, recv, coupling, inner_expand):
    before = lax.ppermute(vec, BLK, UP)
    after = lax.ppermute(vec, BLK, DOWN)
    return pl.pallas_call(
        local_kernel,
        in_specs=[SMEM] + vmem(7),
        out_specs=vmem(1)[0],
        out_shape=shape((2, 16, 512), f32),
        name="local_terms",
    )(index, before, vec, after, near_blocks, recv, coupling, inner_expand)


def group_sums(recv):
    send = pl.pallas_call(
        sum_kernel,
        in_specs=vmem(1),
        out_specs=vmem(1)[0],
        out_shape=shape((32, 16, 128), bf16),
        name="group_sums",
    )(recv)
    return exchange(send, PLANE)


def local(probes, near_blocks, inner_basis, coupling, inner_expand, outer_basis, group_coupling, outer_expand, ranks):
    index = jnp.stack([lax.axis_index(BLK), lax.axis_index(REGION)]).astype(jnp.int32)
    send = pl.pallas_call(
        start_kernel,
        in_specs=[vmem(1)[0], SMEM] + vmem(2),
        out_specs=vmem(1)[0],
        out_shape=shape((32, 32, 128), bf16),
        name="start",
    )(probes, ranks, inner_basis, outer_basis)
    recv = exchange(send, BLK)
    sums = group_sums(recv)
    near = local_terms(index, probes, near_blocks, recv, coupling, inner_expand)
    first, vec, send = pl.pallas_call(
        middle_kernel,
        in_specs=[SMEM] + vmem(4) + [SMEM] + vmem(2),
        out_specs=vmem(3),
        out_shape=[shape((2, 16, 512), f32), shape((2, 16, 512), bf16), shape((32, 32, 128), bf16)],
        name="middle",
    )(index, sums, group_coupling, outer_expand, near, ranks, inner_basis, outer_basis)
    recv = exchange(send, BLK)
    sums = group_sums(recv)
    near = local_terms(index, vec, near_blocks, recv, coupling, inner_expand)
    second = pl.pallas_call(
        last_kernel,
        in_specs=[SMEM] + vmem(4),
        out_specs=vmem(1)[0],
        out_shape=shape((2, 16, 512), f32),
        name="last",
    )(index, sums, group_coupling, outer_expand, near)
    return first, second


def solution(mesh):
    fine = Mesh(mesh.devices.reshape(2, 4, 8, 2, 2), ALL)
    placed = (
        P(None, None, ALL),
        P(None, None, ALL, None),
        P(None, None, ALL),
        P(None, ALL, None),
        P(None, None, ALL),
        P(None, None, ALL),
        P(None, REGION, None),
        P(None, None, ALL),
        P(ALL),
    )
    return jax.shard_map(
        local,
        mesh=fine,
        in_specs=placed,
        out_specs=(P(None, None, ALL), P(None, None, ALL)),
        check_vma=False,
    )
```

```python
import jax
import jax.numpy as jnp
from jax import lax
from jax.experimental import pallas as pl
from jax.experimental.pallas import tpu as pltpu
from jax.sharding import Mesh
from jax.sharding import PartitionSpec as P

REGION = ("yh", "x")
BLK = ("z", "yl", "c")
PLANE = ("yh", "x", "yl", "c")
ALL = REGION + BLK
NT = (((1,), (1,)), ((), ()))
f32 = jnp.float32
bf16 = jnp.bfloat16


def vmem(n):
    return [pl.BlockSpec(memory_space=pltpu.VMEM)] * n


def nt(rows, mat):
    return lax.dot_general(rows, mat, NT, preferred_element_type=f32)


def nn(rows, mat):
    return jnp.dot(rows, mat, preferred_element_type=f32)


def halves(acc, width):
    real = acc[:16, :width] - acc[16:, width:]
    imag = acc[:16, width:] + acc[16:, :width]
    return real, imag


def paired(acc):
    lane = lax.broadcasted_iota(jnp.int32, (16, 128), 1)
    crossed = pltpu.roll(acc[16:], 64, 1)
    return acc[:16] + jnp.where(lane < 64, -crossed, crossed)


def fill_sends(vec, ranks, inner_basis, outer_basis, send):
    coeff = paired(nt(vec, inner_basis[...].reshape(128, 512)))
    lane = lax.broadcasted_iota(jnp.int32, (16, 128), 1)
    rank = jnp.where(lane < 64, lane, lane - 64)
    coeff = jnp.where(rank < ranks[0], coeff, 0.0).astype(bf16)
    real, imag = halves(nt(vec, outer_basis[...].reshape(512, 512)), 256)
    quarters = (real[:, :128], real[:, 128:], imag[:, :128], imag[:, 128:])
    quarters = [q.astype(bf16) for q in quarters]
    for d in range(32):
        send[d, :16] = coeff
        send[d, 16:] = quarters[d % 4]


def start_kernel(probes, inner_basis, outer_basis, ranks, send):
    fill_sends(probes[...].reshape(32, 512), ranks, inner_basis, outer_basis, send)


def sum_kernel(recv, before, after, send):
    total = recv[0, 16:].astype(f32)
    for j in range(1, 32):
        total = total + recv[j, 16:].astype(f32)
    total = total.astype(bf16)
    for d in range(32):
        send[d] = total


def local_kernel(before, vec, after, recv, near_blocks, coupling, inner_expand, out):
    acc = None
    for b, part in enumerate((before, vec, after)):
        term = nt(part[...].reshape(32, 512), near_blocks[b].reshape(1024, 512))
        acc = term if acc is None else acc + term
    real, imag = halves(acc, 512)
    lane = lax.broadcasted_iota(jnp.int32, (16, 128), 1)
    position = lax.axis_index(BLK)
    res, ims = [], []
    for j in range(0, 32, 2):
        first, second = (
            jnp.where(jnp.abs(k - position) > 1, recv[k, :16].astype(f32), 0.0) for k in (j, j + 1)
        )
        res.append(jnp.where(lane < 64, first, pltpu.roll(second, 64, 1)))
        ims.append(jnp.where(lane < 64, pltpu.roll(first, 64, 1), second))
    rows = jnp.concatenate([jnp.concatenate(res, 1), jnp.concatenate(ims, 1)], 0).astype(bf16)
    inner = paired(nt(rows, coupling[...].reshape(128, 2048)))
    rows = jnp.concatenate([inner[:, :64], pltpu.roll(inner, 64, 1)[:, :64]], 0).astype(bf16)
    a, b = nn(rows, inner_expand[0]), nn(rows, inner_expand[1])
    out[0] = real + (a[:16] - b[16:])
    out[1] = imag + (a[16:] + b[:16])


def field_part(recv, coupling, expand):
    region = lax.axis_index(REGION)
    res, ims = [], []
    for s in range(8):
        tiles = [jnp.where(s != region, recv[4 * s + q], jnp.zeros((16, 128), bf16)) for q in range(4)]
        res += tiles[:2]
        ims += tiles[2:]
    rows = jnp.concatenate([jnp.concatenate(res, 1), jnp.concatenate(ims, 1)], 0)
    real, imag = halves(nt(rows, coupling[...].reshape(512, 2048)), 256)
    rows = jnp.concatenate([real, imag], 0).astype(bf16)
    a, b = nn(rows, expand[0]), nn(rows, expand[1])
    return a[:16] - b[16:], a[16:] + b[:16]


def middle_kernel(recv, coupling, expand, local, inner_hbm, outer_hbm, ranks, first, vec, send, *scratch):
    inner_basis, outer_basis, sems = scratch
    copies = [
        pltpu.make_async_copy(inner_hbm, inner_basis, sems.at[0]),
        pltpu.make_async_copy(outer_hbm, outer_basis, sems.at[1]),
    ]
    for copy in copies:
        copy.start()
    real, imag = field_part(recv, coupling, expand)
    real, imag = local[0] + real, local[1] + imag
    first[0] = real
    first[1] = imag
    rows = jnp.concatenate([real, imag], 0).astype(bf16)
    vec[0] = rows[:16]
    vec[1] = rows[16:]
    for copy in copies:
        copy.wait()
    fill_sends(rows, ranks, inner_basis, outer_basis, send)


def last_kernel(recv, coupling, expand, local, second):
    real, imag = field_part(recv, coupling, expand)
    second[0] = local[0] + real
    second[1] = local[1] + imag


UP = [(i, i + 1) for i in range(31)]
DOWN = [(i + 1, i) for i in range(31)]
ANY = pl.BlockSpec(memory_space=pl.ANY)
RANKS = pl.BlockSpec(memory_space=pltpu.SMEM)
PARAMS = pltpu.CompilerParams(vmem_limit_bytes=16 * 1024 * 1024)


def in_vmem(*arrays):
    return [pltpu.with_memory_space_constraint(a, pltpu.VMEM) for a in arrays]


def in_hbm(*arrays):
    return [pltpu.with_memory_space_constraint(a, pltpu.HBM) for a in arrays]


def call(kernel, outs, *args):
    return pl.pallas_call(
        kernel,
        in_specs=[RANKS if a.dtype == jnp.int32 else vmem(1)[0] for a in args],
        out_specs=vmem(len(outs)),
        out_shape=outs,
        compiler_params=PARAMS,
    )(*args)


def exchange(value, axes):
    return lax.all_to_all(value, axes, split_axis=0, concat_axis=0, tiled=True)


def neighbours(vec):
    return lax.ppermute(vec, BLK, UP), lax.ppermute(vec, BLK, DOWN)


def local_terms(before, vec, after, recv, near_blocks, coupling, inner_expand):
    args = in_vmem(before) + [vec] + in_vmem(after, recv) + in_hbm(near_blocks, coupling, inner_expand)
    return call(local_kernel, [pltpu.VMEM((2, 16, 512), f32)], *args)[0]


def group_sums(recv, before, after):
    send = pl.pallas_call(
        sum_kernel,
        in_specs=vmem(1) + [ANY] * 2,
        out_specs=vmem(1)[0],
        out_shape=pltpu.VMEM((32, 16, 128), bf16),
        compiler_params=PARAMS,
        name="group_sums",
    )(*in_vmem(recv), before, after)
    return exchange(send, PLANE)


def local(probes, near_blocks, inner_basis, coupling, inner_expand, outer_basis, group_coupling, outer_expand, ranks):
    sends = pltpu.VMEM((32, 32, 128), bf16)
    send = call(start_kernel, [sends], *in_hbm(probes, inner_basis, outer_basis), ranks)[0]
    recv = exchange(send, BLK)
    before, after = neighbours(probes)
    probes = in_hbm(probes)[0]
    sums = group_sums(recv, before, after)
    near = local_terms(before, probes, after, recv, near_blocks, coupling, inner_expand)
    outs = [pltpu.VMEM((2, 16, 512), f32), pltpu.VMEM((2, 16, 512), bf16), sends]
    weights = in_vmem(group_coupling, outer_expand)
    first, vec, send = pl.pallas_call(
        middle_kernel,
        in_specs=vmem(4) + [ANY] * 2 + [RANKS],
        out_specs=vmem(3),
        out_shape=outs,
        scratch_shapes=[
            pltpu.VMEM(inner_basis.shape, bf16),
            pltpu.VMEM(outer_basis.shape, bf16),
            pltpu.SemaphoreType.DMA((2,)),
        ],
        compiler_params=PARAMS,
        name="middle",
    )(*in_vmem(sums), *weights, *in_vmem(near), *in_hbm(inner_basis, outer_basis), ranks)
    recv = exchange(send, BLK)
    before, after = neighbours(vec)
    sums = group_sums(recv, before, after)
    vec = in_vmem(vec)[0]
    near = local_terms(before, vec, after, recv, near_blocks, coupling, inner_expand)
    args = in_vmem(sums) + weights + in_vmem(near)
    second = call(last_kernel, [jax.ShapeDtypeStruct((2, 16, 512), f32)], *args)[0]
    return first, second


def solution(mesh):
    fine = Mesh(mesh.devices.reshape(2, 4, 8, 2, 2), ALL)
    placed = (
        P(None, None, ALL),
        P(None, None, ALL, None),
        P(None, None, ALL),
        P(None, ALL, None),
        P(None, None, ALL),
        P(None, None, ALL),
        P(None, REGION, None),
        P(None, None, ALL),
        P(ALL),
    )
    return jax.shard_map(
        local,
        mesh=fine,
        in_specs=placed,
        out_specs=(P(None, None, ALL), P(None, None, ALL)),
        check_vma=False,
    )
```

```python
import jax
import jax.numpy as jnp
from jax import lax
from jax.experimental import pallas as pl
from jax.experimental.pallas import tpu as pltpu
from jax.sharding import Mesh
from jax.sharding import PartitionSpec as P

REGION = ("yh", "x")
BLK = ("z", "yl", "c")
CHIPS = ("z", "yl")
PLANE = ("yh", "x", "yl", "c")
ALL = REGION + BLK
NT = (((1,), (1,)), ((), ()))
f32 = jnp.float32
bf16 = jnp.bfloat16


def vmem(n):
    return [pl.BlockSpec(memory_space=pltpu.VMEM)] * n


def nt(rows, mat):
    return lax.dot_general(rows, mat, NT, preferred_element_type=f32)


def nn(rows, mat):
    return jnp.dot(rows, mat, preferred_element_type=f32)


def halves(acc, width):
    real = acc[:16, :width] - acc[16:, width:]
    imag = acc[:16, width:] + acc[16:, :width]
    return real, imag


def paired(acc):
    lane = lax.broadcasted_iota(jnp.int32, (16, 128), 1)
    crossed = pltpu.roll(acc[16:], 64, 1)
    return acc[:16] + jnp.where(lane < 64, -crossed, crossed)


def fill_pair(vec, ranks, inner_basis, outer_basis, give, keep):
    coeff = paired(nt(vec, inner_basis[...].reshape(128, 512)))
    lane = lax.broadcasted_iota(jnp.int32, (16, 128), 1)
    rank = jnp.where(lane < 64, lane, lane - 64)
    coeff = jnp.where(rank < ranks[0], coeff, 0.0)
    real, imag = halves(nt(vec, outer_basis[...].reshape(512, 512)), 256)
    core = lax.axis_index("c")
    wide = jnp.concatenate([real, imag], 0)
    low, high = wide[:, :128], wide[:, 128:]
    keep[:16] = coeff.astype(bf16).astype(f32)
    keep[16:] = jnp.where(core == 0, low, high)
    give[:16] = coeff.astype(bf16)
    give[16:48] = jnp.where(core == 0, high, low).astype(bf16)
    for k in range(4):
        give[48 + 32 * k : 80 + 32 * k] = vec[:, 128 * k : 128 * k + 128]


def start_kernel(probes, inner_basis, outer_basis, ranks, give, keep):
    fill_pair(probes[...].reshape(32, 512), ranks, inner_basis, outer_basis, give, keep)


def pair_kernel(got, keep, send):
    core = lax.axis_index("c")
    mine, other = keep[:16].astype(bf16), got[:16]
    even, odd = jnp.where(core == 0, mine, other), jnp.where(core == 0, other, mine)
    quarters = (keep[16:] + got[16:48].astype(f32)).astype(bf16)
    for d in range(16):
        part = d % 2
        send[d, :16] = even
        send[d, 16:32] = odd
        send[d, 32:] = quarters[16 * part : 16 * part + 16]


def sum_kernel(recv, cross, send):
    total = recv[0, 32:].astype(f32)
    for j in range(1, 16):
        total = total + recv[j, 32:].astype(f32)
    total = total.astype(bf16)
    for d in range(32):
        send[d] = total


def local_kernel(got, cross, vec, recv, near_blocks, coupling, inner_expand, out):
    core = lax.axis_index("c")
    partner = jnp.concatenate([got[48 + 32 * k : 80 + 32 * k] for k in range(4)], 1)
    cross = cross[...].reshape(32, 512)
    before, after = jnp.where(core == 0, cross, partner), jnp.where(core == 0, partner, cross)
    acc = None
    for b, part in enumerate((before, vec[...].reshape(32, 512), after)):
        term = nt(part, near_blocks[b].reshape(1024, 512))
        acc = term if acc is None else acc + term
    real, imag = halves(acc, 512)
    lane = lax.broadcasted_iota(jnp.int32, (16, 128), 1)
    position = lax.axis_index(BLK)
    res, ims = [], []
    for j in range(16):
        first, second = (
            jnp.where(jnp.abs(2 * j + k - position) > 1, recv[j, 16 * k : 16 * k + 16].astype(f32), 0.0)
            for k in range(2)
        )
        res.append(jnp.where(lane < 64, first, pltpu.roll(second, 64, 1)))
        ims.append(jnp.where(lane < 64, pltpu.roll(first, 64, 1), second))
    rows = jnp.concatenate([jnp.concatenate(res, 1), jnp.concatenate(ims, 1)], 0).astype(bf16)
    inner = paired(nt(rows, coupling[...].reshape(128, 2048)))
    rows = jnp.concatenate([inner[:, :64], pltpu.roll(inner, 64, 1)[:, :64]], 0).astype(bf16)
    a, b = nn(rows, inner_expand[0]), nn(rows, inner_expand[1])
    out[0] = real + (a[:16] - b[16:])
    out[1] = imag + (a[16:] + b[:16])


def field_part(recv, coupling, expand):
    region = lax.axis_index(REGION)
    res, ims = [], []
    for s in range(8):
        tiles = [jnp.where(s != region, recv[4 * s + q], jnp.zeros((16, 128), bf16)) for q in range(4)]
        res += tiles[:2]
        ims += tiles[2:]
    rows = jnp.concatenate([jnp.concatenate(res, 1), jnp.concatenate(ims, 1)], 0)
    real, imag = halves(nt(rows, coupling[...].reshape(512, 2048)), 256)
    rows = jnp.concatenate([real, imag], 0).astype(bf16)
    a, b = nn(rows, expand[0]), nn(rows, expand[1])
    return a[:16] - b[16:], a[16:] + b[:16]


def middle_kernel(recv, coupling, expand, local, inner_hbm, outer_hbm, ranks, first, vec, give, keep, *scratch):
    inner_basis, outer_basis, sems = scratch
    copies = [
        pltpu.make_async_copy(inner_hbm, inner_basis, sems.at[0]),
        pltpu.make_async_copy(outer_hbm, outer_basis, sems.at[1]),
    ]
    for copy in copies:
        copy.start()
    real, imag = field_part(recv, coupling, expand)
    real, imag = local[0] + real, local[1] + imag
    first[0] = real
    first[1] = imag
    rows = jnp.concatenate([real, imag], 0).astype(bf16)
    vec[0] = rows[:16]
    vec[1] = rows[16:]
    for copy in copies:
        copy.wait()
    fill_pair(rows, ranks, inner_basis, outer_basis, give, keep)


def last_kernel(recv, coupling, expand, local, second):
    real, imag = field_part(recv, coupling, expand)
    second[0] = local[0] + real
    second[1] = local[1] + imag


PARTNER = [(i, i ^ 1) for i in range(32)]
CROSS = [(i, i + 1) for i in range(1, 31, 2)] + [(i, i - 1) for i in range(2, 32, 2)]
ANY = pl.BlockSpec(memory_space=pl.ANY)
RANKS = pl.BlockSpec(memory_space=pltpu.SMEM)
PARAMS = pltpu.CompilerParams(vmem_limit_bytes=16 * 1024 * 1024)


def in_vmem(*arrays):
    return [pltpu.with_memory_space_constraint(a, pltpu.VMEM) for a in arrays]


def in_hbm(*arrays):
    return [pltpu.with_memory_space_constraint(a, pltpu.HBM) for a in arrays]


def call(kernel, outs, *args):
    return pl.pallas_call(
        kernel,
        in_specs=[RANKS if a.dtype == jnp.int32 else vmem(1)[0] for a in args],
        out_specs=vmem(len(outs)),
        out_shape=outs,
        compiler_params=PARAMS,
    )(*args)


def exchange(value, axes):
    return lax.all_to_all(value, axes, split_axis=0, concat_axis=0, tiled=True)


def swapped(give, keep):
    got = lax.ppermute(give, BLK, PARTNER)
    args = in_vmem(got, keep)
    return got, call(pair_kernel, [pltpu.VMEM((16, 48, 128), bf16)], *args)[0]


def crossed(vec):
    return lax.ppermute(vec, BLK, CROSS)


def local_terms(got, cross, vec, recv, near_blocks, coupling, inner_expand):
    args = in_vmem(got, cross) + [vec] + in_vmem(recv) + in_hbm(near_blocks, coupling, inner_expand)
    return call(local_kernel, [pltpu.VMEM((2, 16, 512), f32)], *args)[0]


def group_sums(recv, cross):
    send = pl.pallas_call(
        sum_kernel,
        in_specs=vmem(1) + [ANY],
        out_specs=vmem(1)[0],
        out_shape=pltpu.VMEM((32, 16, 128), bf16),
        compiler_params=PARAMS,
        name="group_sums",
    )(*in_vmem(recv), cross)
    return exchange(send, PLANE)


def local(probes, near_blocks, inner_basis, coupling, inner_expand, outer_basis, group_coupling, outer_expand, ranks):
    pair = [pltpu.VMEM((176, 128), bf16), pltpu.VMEM((48, 128), f32)]
    give, keep = call(start_kernel, pair, *in_hbm(probes, inner_basis, outer_basis), ranks)
    got, send = swapped(give, keep)
    recv = exchange(send, CHIPS)
    cross = crossed(probes)
    sums = group_sums(recv, cross)
    near = local_terms(got, cross, *in_hbm(probes), recv, near_blocks, coupling, inner_expand)
    outs = [pltpu.VMEM((2, 16, 512), f32), pltpu.VMEM((2, 16, 512), bf16)] + pair
    weights = in_vmem(group_coupling, outer_expand)
    first, vec, give, keep = pl.pallas_call(
        middle_kernel,
        in_specs=vmem(4) + [ANY] * 2 + [RANKS],
        out_specs=vmem(4),
        out_shape=outs,
        scratch_shapes=[
            pltpu.VMEM(inner_basis.shape, bf16),
            pltpu.VMEM(outer_basis.shape, bf16),
            pltpu.SemaphoreType.DMA((2,)),
        ],
        compiler_params=PARAMS,
        name="middle",
    )(*in_vmem(sums), *weights, *in_vmem(near), *in_hbm(inner_basis, outer_basis), ranks)
    got, send = swapped(give, keep)
    recv = exchange(send, CHIPS)
    cross = crossed(vec)
    sums = group_sums(recv, cross)
    near = local_terms(got, cross, *in_vmem(vec), recv, near_blocks, coupling, inner_expand)
    args = in_vmem(sums) + weights + in_vmem(near)
    second = call(last_kernel, [jax.ShapeDtypeStruct((2, 16, 512), f32)], *args)[0]
    return first, second


def solution(mesh):
    fine = Mesh(mesh.devices.reshape(2, 4, 8, 2, 2), ALL)
    placed = (
        P(None, None, ALL),
        P(None, None, ALL, None),
        P(None, None, ALL),
        P(None, ALL, None),
        P(None, None, ALL),
        P(None, None, ALL),
        P(None, REGION, None),
        P(None, None, ALL),
        P(ALL),
    )
    return jax.shard_map(
        local,
        mesh=fine,
        in_specs=placed,
        out_specs=(P(None, None, ALL), P(None, None, ALL)),
        check_vma=False,
    )
```

```python
import jax
import jax.numpy as jnp
from jax import lax
from jax.experimental import pallas as pl
from jax.experimental.pallas import tpu as pltpu
from jax.sharding import Mesh
from jax.sharding import PartitionSpec as P

REGION = ("yh", "x")
BLK = ("z", "yl", "c")
CHIPS = ("z", "yl")
PLANE = ("yh", "x", "yl", "c")
ALL = REGION + BLK
NT = (((1,), (1,)), ((), ()))
f32 = jnp.float32
bf16 = jnp.bfloat16


def vmem(n):
    return [pl.BlockSpec(memory_space=pltpu.VMEM)] * n


def nt(rows, mat):
    return lax.dot_general(rows, mat, NT, preferred_element_type=f32)


def nn(rows, mat):
    return jnp.dot(rows, mat, preferred_element_type=f32)


def halves(acc, width):
    real = acc[:16, :width] - acc[16:, width:]
    imag = acc[:16, width:] + acc[16:, :width]
    return real, imag


def paired(acc):
    lane = lax.broadcasted_iota(jnp.int32, (16, 128), 1)
    crossed = pltpu.roll(acc[16:], 64, 1)
    return acc[:16] + jnp.where(lane < 64, -crossed, crossed)


def fill_pair(vec, inner_basis, outer_basis, give, keep):
    real, imag = halves(nt(vec, outer_basis[...].reshape(512, 512)), 256)
    core = lax.axis_index("c")
    wide = jnp.concatenate([real, imag], 0)
    low, high = wide[:, :128], wide[:, 128:]
    keep[:16] = paired(nt(vec, inner_basis[...].reshape(128, 512)))
    keep[16:] = jnp.where(core == 0, low, high)
    give[:32] = jnp.where(core == 0, high, low).astype(bf16)
    for k in range(4):
        give[32 + 32 * k : 64 + 32 * k] = vec[:, 128 * k : 128 * k + 128]


def start_kernel(probes, inner_basis, outer_basis, give, keep):
    fill_pair(probes[...].reshape(32, 512), inner_basis, outer_basis, give, keep)


def pair_kernel(got, keep, ranks, send):
    lane = lax.broadcasted_iota(jnp.int32, (16, 128), 1)
    rank = jnp.where(lane < 64, lane, lane - 64)
    coeff = jnp.where(rank < ranks[0], keep[:16], 0.0).astype(bf16)
    quarters = (keep[16:] + got[:32].astype(f32)).astype(bf16)
    for d in range(16):
        part = d % 2
        send[d, :16] = coeff
        send[d, 16:] = quarters[16 * part : 16 * part + 16]


def sum_kernel(recv, send):
    total = recv[0, 16:].astype(f32)
    for j in range(1, 16):
        total = total + recv[j, 16:].astype(f32)
    total = total.astype(bf16)
    for d in range(32):
        send[d] = total


def near_kernel(got, vec, blocks_hbm, out, blocks, sems):
    other = 2 - 2 * lax.axis_index("c")
    copies = [
        pltpu.make_async_copy(blocks_hbm.at[source], blocks.at[slot], sems.at[slot])
        for slot, source in enumerate((1, other))
    ]
    for copy in copies:
        copy.start()
    partner = jnp.concatenate([got[32 + 32 * k : 64 + 32 * k] for k in range(4)], 1)
    copies[0].wait()
    acc = nt(vec[...].reshape(32, 512), blocks[0].reshape(1024, 512))
    copies[1].wait()
    acc = acc + nt(partner, blocks[1].reshape(1024, 512))
    out[0], out[1] = halves(acc, 512)


def terms_kernel(near, cross, recv, other, blocks_hbm, coupling_hbm, expand_hbm, out, block, coupling, expand, sems):
    core = lax.axis_index("c")
    copies = [
        pltpu.make_async_copy(coupling_hbm, coupling, sems.at[0]),
        pltpu.make_async_copy(expand_hbm, expand, sems.at[1]),
        pltpu.make_async_copy(blocks_hbm.at[2 * core], block, sems.at[2]),
    ]
    for copy in copies:
        copy.start()
    lane = lax.broadcasted_iota(jnp.int32, (16, 128), 1)
    position = lax.axis_index(BLK)
    res, ims = [], []
    for j in range(16):
        mine, theirs = (ref[j, :16].astype(f32) for ref in (recv, other))
        first, second = jnp.where(core == 0, mine, theirs), jnp.where(core == 0, theirs, mine)
        first = jnp.where(jnp.abs(2 * j - position) > 1, first, 0.0)
        second = jnp.where(jnp.abs(2 * j + 1 - position) > 1, second, 0.0)
        res.append(jnp.where(lane < 64, first, pltpu.roll(second, 64, 1)))
        ims.append(jnp.where(lane < 64, pltpu.roll(first, 64, 1), second))
    rows = jnp.concatenate([jnp.concatenate(res, 1), jnp.concatenate(ims, 1)], 0).astype(bf16)
    copies[0].wait()
    inner = paired(nt(rows, coupling[...].reshape(128, 2048)))
    rows = jnp.concatenate([inner[:, :64], pltpu.roll(inner, 64, 1)[:, :64]], 0).astype(bf16)
    copies[1].wait()
    a, b = nn(rows, expand[0]), nn(rows, expand[1])
    copies[2].wait()
    real, imag = halves(nt(cross[...].reshape(32, 512), block[...].reshape(1024, 512)), 512)
    out[0] = near[0] + real + (a[:16] - b[16:])
    out[1] = near[1] + imag + (a[16:] + b[:16])


def field_part(recv, coupling, expand):
    region = lax.axis_index(REGION)
    res, ims = [], []
    for s in range(8):
        tiles = [jnp.where(s != region, recv[4 * s + q], jnp.zeros((16, 128), bf16)) for q in range(4)]
        res += tiles[:2]
        ims += tiles[2:]
    rows = jnp.concatenate([jnp.concatenate(res, 1), jnp.concatenate(ims, 1)], 0)
    real, imag = halves(nt(rows, coupling[...].reshape(512, 2048)), 256)
    rows = jnp.concatenate([real, imag], 0).astype(bf16)
    a, b = nn(rows, expand[0]), nn(rows, expand[1])
    return a[:16] - b[16:], a[16:] + b[:16]


def middle_kernel(recv, coupling, expand, local, inner_hbm, outer_hbm, first_hbm, vec, give, keep, *scratch):
    inner_basis, outer_basis, first, sems = scratch
    copies = [
        pltpu.make_async_copy(inner_hbm, inner_basis, sems.at[0]),
        pltpu.make_async_copy(outer_hbm, outer_basis, sems.at[1]),
    ]
    for copy in copies:
        copy.start()
    real, imag = field_part(recv, coupling, expand)
    real, imag = local[0] + real, local[1] + imag
    first[0] = real
    first[1] = imag
    result = pltpu.make_async_copy(first, first_hbm, sems.at[2])
    result.start()
    rows = jnp.concatenate([real, imag], 0).astype(bf16)
    vec[0] = rows[:16]
    vec[1] = rows[16:]
    for copy in copies:
        copy.wait()
    fill_pair(rows, inner_basis, outer_basis, give, keep)
    result.wait()


def last_kernel(recv, coupling, expand, local, second):
    real, imag = field_part(recv, coupling, expand)
    second[0] = local[0] + real
    second[1] = local[1] + imag


PARTNER = [(i, i ^ 1) for i in range(32)]
CROSS = [(i, i + 1) for i in range(1, 31, 2)] + [(i, i - 1) for i in range(2, 32, 2)]
ANY = pl.BlockSpec(memory_space=pl.ANY)
RANKS = pl.BlockSpec(memory_space=pltpu.SMEM)
PARAMS = pltpu.CompilerParams(vmem_limit_bytes=16 * 1024 * 1024)


def in_vmem(*arrays):
    return [pltpu.with_memory_space_constraint(a, pltpu.VMEM) for a in arrays]


def in_hbm(*arrays):
    return [pltpu.with_memory_space_constraint(a, pltpu.HBM) for a in arrays]


def call(kernel, outs, *args):
    return pl.pallas_call(
        kernel,
        in_specs=vmem(len(args)),
        out_specs=vmem(len(outs)),
        out_shape=outs,
        compiler_params=PARAMS,
    )(*args)


def exchange(value, axes):
    return lax.all_to_all(value, axes, split_axis=0, concat_axis=0, tiled=True)


def swapped(give, keep, ranks):
    got = lax.ppermute(give, BLK, PARTNER)
    send = pl.pallas_call(
        pair_kernel,
        in_specs=vmem(2) + [RANKS],
        out_specs=vmem(1)[0],
        out_shape=pltpu.VMEM((16, 32, 128), bf16),
        compiler_params=PARAMS,
        name="pair_sums",
    )(*in_vmem(got, keep), ranks)
    return got, send


def crossed(vec):
    return lax.ppermute(vec, BLK, CROSS)


def near_terms(got, vec, near_blocks):
    return pl.pallas_call(
        near_kernel,
        in_specs=vmem(2) + [ANY],
        out_specs=vmem(1)[0],
        out_shape=pltpu.VMEM((2, 16, 512), f32),
        scratch_shapes=[pltpu.VMEM((2, 2, 512, 512), bf16), pltpu.SemaphoreType.DMA((2,))],
        compiler_params=PARAMS,
        name="near_terms",
    )(*in_vmem(got), vec, *in_hbm(near_blocks))


def local_terms(near, cross, recv, near_blocks, coupling, inner_expand):
    other = lax.ppermute(recv, BLK, PARTNER)
    return pl.pallas_call(
        terms_kernel,
        in_specs=vmem(4) + [ANY] * 3,
        out_specs=vmem(1)[0],
        out_shape=pltpu.VMEM((2, 16, 512), f32),
        scratch_shapes=[
            pltpu.VMEM((2, 512, 512), bf16),
            pltpu.VMEM(coupling.shape, bf16),
            pltpu.VMEM(inner_expand.shape, bf16),
            pltpu.SemaphoreType.DMA((3,)),
        ],
        compiler_params=PARAMS,
        name="local_terms",
    )(*in_vmem(near, cross, recv, other), *in_hbm(near_blocks, coupling, inner_expand))


def group_sums(recv):
    send = call(sum_kernel, [pltpu.VMEM((32, 16, 128), bf16)], *in_vmem(recv))[0]
    return exchange(send, PLANE)


def local(probes, near_blocks, inner_basis, coupling, inner_expand, outer_basis, group_coupling, outer_expand, ranks):
    pair = [pltpu.VMEM((160, 128), bf16), pltpu.VMEM((48, 128), f32)]
    give, keep = pl.pallas_call(
        start_kernel,
        in_specs=vmem(3),
        out_specs=vmem(2),
        out_shape=pair,
        compiler_params=PARAMS,
        name="start",
    )(*in_hbm(probes, inner_basis, outer_basis))
    got, send = swapped(give, keep, ranks)
    recv = exchange(send, CHIPS)
    cross = crossed(probes)
    sums = group_sums(recv)
    near = near_terms(got, *in_hbm(probes), near_blocks)
    near = local_terms(near, cross, recv, near_blocks, coupling, inner_expand)
    outs = [jax.ShapeDtypeStruct((2, 16, 512), f32), pltpu.VMEM((2, 16, 512), bf16)] + pair
    weights = in_vmem(group_coupling, outer_expand)
    first, vec, give, keep = pl.pallas_call(
        middle_kernel,
        in_specs=vmem(4) + [ANY] * 2,
        out_specs=[ANY] + vmem(3),
        out_shape=outs,
        scratch_shapes=[
            pltpu.VMEM(inner_basis.shape, bf16),
            pltpu.VMEM(outer_basis.shape, bf16),
            pltpu.VMEM((2, 16, 512), f32),
            pltpu.SemaphoreType.DMA((3,)),
        ],
        compiler_params=PARAMS,
        name="middle",
    )(*in_vmem(sums), *weights, *in_vmem(near), *in_hbm(inner_basis, outer_basis))
    got, send = swapped(give, keep, ranks)
    recv = exchange(send, CHIPS)
    cross = crossed(vec)
    sums = group_sums(recv)
    near = near_terms(got, *in_vmem(vec), near_blocks)
    near = local_terms(near, cross, recv, near_blocks, coupling, inner_expand)
    args = in_vmem(sums) + weights + in_vmem(near)
    second = call(last_kernel, [jax.ShapeDtypeStruct((2, 16, 512), f32)], *args)[0]
    return first, second


def solution(mesh):
    fine = Mesh(mesh.devices.reshape(2, 4, 8, 2, 2), ALL)
    placed = (
        P(None, None, ALL),
        P(None, None, ALL, None),
        P(None, None, ALL),
        P(None, ALL, None),
        P(None, None, ALL),
        P(None, None, ALL),
        P(None, REGION, None),
        P(None, None, ALL),
        P(ALL),
    )
    return jax.shard_map(
        local,
        mesh=fine,
        in_specs=placed,
        out_specs=(P(None, None, ALL), P(None, None, ALL)),
        check_vma=False,
    )
```

```python
import jax
import jax.numpy as jnp
from jax import lax
from jax.experimental import pallas as pl
from jax.experimental.pallas import tpu as pltpu
from jax.sharding import PartitionSpec as P

ALL = ("region", "blk")
CHIP_ORDER = tuple(2 * z + y for z in (4, 5, 6, 7, 3, 2, 1, 0) for y in (1, 0))
CHIPS = [[32 * r + 2 * i + c for i in CHIP_ORDER] for r in range(8) for c in range(2)]
PLANE = [[32 * r + 4 * z + q for r in range(8) for q in range(4)] for z in range(8)]
PARTNER = [(d, d ^ 1) for d in range(256)]
CROSS = [(d, d + 1) for d in range(256) if d % 2 == 1 and d % 32 != 31]
CROSS += [(d, d - 1) for d in range(256) if d % 2 == 0 and d % 32 != 0]
NT = (((1,), (1,)), ((), ()))
f32 = jnp.float32
bf16 = jnp.bfloat16


def vmem(n):
    return [pl.BlockSpec(memory_space=pltpu.VMEM)] * n


def nt(rows, mat):
    return lax.dot_general(rows, mat, NT, preferred_element_type=f32)


def nn(rows, mat):
    return jnp.dot(rows, mat, preferred_element_type=f32)


def halves(acc, width):
    real = acc[:16, :width] - acc[16:, width:]
    imag = acc[:16, width:] + acc[16:, :width]
    return real, imag


def paired(acc):
    lane = lax.broadcasted_iota(jnp.int32, (16, 128), 1)
    crossed = pltpu.roll(acc[16:], 64, 1)
    return acc[:16] + jnp.where(lane < 64, -crossed, crossed)


def fill_pair(vec, inner_basis, outer_basis, give, keep):
    real, imag = halves(nt(vec, outer_basis[...].reshape(512, 512)), 256)
    core = lax.rem(lax.axis_index("blk"), 2)
    wide = jnp.concatenate([real, imag], 0)
    low, high = wide[:, :128], wide[:, 128:]
    keep[:16] = paired(nt(vec, inner_basis[...].reshape(128, 512)))
    keep[16:] = jnp.where(core == 0, low, high)
    give[:32] = jnp.where(core == 0, high, low).astype(bf16)
    for k in range(4):
        give[32 + 32 * k : 64 + 32 * k] = vec[:, 128 * k : 128 * k + 128]


def start_kernel(probes, inner_basis, outer_basis, give, keep):
    fill_pair(probes[...].reshape(32, 512), inner_basis, outer_basis, give, keep)


def pair_kernel(got, keep, ranks, send):
    lane = lax.broadcasted_iota(jnp.int32, (16, 128), 1)
    rank = jnp.where(lane < 64, lane, lane - 64)
    coeff = jnp.where(rank < ranks[0], keep[:16], 0.0).astype(bf16)
    quarters = (keep[16:] + got[:32].astype(f32)).astype(bf16)
    for d in range(16):
        part = CHIP_ORDER[d] % 2
        send[d, :16] = coeff
        send[d, 16:] = quarters[16 * part : 16 * part + 16]


def sum_kernel(recv, send):
    total = recv[0, 16:].astype(f32)
    for j in range(1, 16):
        total = total + recv[j, 16:].astype(f32)
    total = total.astype(bf16)
    for d in range(32):
        send[d] = total


def near_kernel(got, vec, blocks_hbm, out, blocks, sems):
    other = 2 - 2 * lax.rem(lax.axis_index("blk"), 2)
    copies = [
        pltpu.make_async_copy(blocks_hbm.at[source], blocks.at[slot], sems.at[slot])
        for slot, source in enumerate((1, other))
    ]
    for copy in copies:
        copy.start()
    partner = jnp.concatenate([got[32 + 32 * k : 64 + 32 * k] for k in range(4)], 1)
    copies[0].wait()
    acc = nt(vec[...].reshape(32, 512), blocks[0].reshape(1024, 512))
    copies[1].wait()
    acc = acc + nt(partner, blocks[1].reshape(1024, 512))
    out[0], out[1] = halves(acc, 512)


def terms_kernel(near, cross, recv, other, blocks_hbm, coupling_hbm, expand_hbm, out, block, coupling, expand, sems):
    core = lax.rem(lax.axis_index("blk"), 2)
    copies = [
        pltpu.make_async_copy(coupling_hbm, coupling, sems.at[0]),
        pltpu.make_async_copy(expand_hbm, expand, sems.at[1]),
        pltpu.make_async_copy(blocks_hbm.at[2 * core], block, sems.at[2]),
    ]
    for copy in copies:
        copy.start()
    lane = lax.broadcasted_iota(jnp.int32, (16, 128), 1)
    position = lax.axis_index("blk")
    res, ims = [], []
    for j in range(16):
        mine, theirs = (ref[CHIP_ORDER.index(j), :16].astype(f32) for ref in (recv, other))
        first, second = jnp.where(core == 0, mine, theirs), jnp.where(core == 0, theirs, mine)
        first = jnp.where(jnp.abs(2 * j - position) > 1, first, 0.0)
        second = jnp.where(jnp.abs(2 * j + 1 - position) > 1, second, 0.0)
        res.append(jnp.where(lane < 64, first, pltpu.roll(second, 64, 1)))
        ims.append(jnp.where(lane < 64, pltpu.roll(first, 64, 1), second))
    rows = jnp.concatenate([jnp.concatenate(res, 1), jnp.concatenate(ims, 1)], 0).astype(bf16)
    copies[0].wait()
    inner = paired(nt(rows, coupling[...].reshape(128, 2048)))
    rows = jnp.concatenate([inner[:, :64], pltpu.roll(inner, 64, 1)[:, :64]], 0).astype(bf16)
    copies[1].wait()
    a, b = nn(rows, expand[0]), nn(rows, expand[1])
    copies[2].wait()
    real, imag = halves(nt(cross[...].reshape(32, 512), block[...].reshape(1024, 512)), 512)
    out[0] = near[0] + real + (a[:16] - b[16:])
    out[1] = near[1] + imag + (a[16:] + b[:16])


def field_part(recv, coupling, expand):
    region = lax.axis_index("region")
    res, ims = [], []
    for s in range(8):
        tiles = [jnp.where(s != region, recv[4 * s + q], jnp.zeros((16, 128), bf16)) for q in range(4)]
        res += tiles[:2]
        ims += tiles[2:]
    rows = jnp.concatenate([jnp.concatenate(res, 1), jnp.concatenate(ims, 1)], 0)
    real, imag = halves(nt(rows, coupling[...].reshape(512, 2048)), 256)
    rows = jnp.concatenate([real, imag], 0).astype(bf16)
    a, b = nn(rows, expand[0]), nn(rows, expand[1])
    return a[:16] - b[16:], a[16:] + b[:16]


def middle_kernel(recv, coupling, expand, local, inner_hbm, outer_hbm, first_hbm, vec, give, keep, *scratch):
    inner_basis, outer_basis, first, sems = scratch
    copies = [
        pltpu.make_async_copy(inner_hbm, inner_basis, sems.at[0]),
        pltpu.make_async_copy(outer_hbm, outer_basis, sems.at[1]),
    ]
    for copy in copies:
        copy.start()
    real, imag = field_part(recv, coupling, expand)
    real, imag = local[0] + real, local[1] + imag
    first[0] = real
    first[1] = imag
    result = pltpu.make_async_copy(first, first_hbm, sems.at[2])
    result.start()
    rows = jnp.concatenate([real, imag], 0).astype(bf16)
    vec[0] = rows[:16]
    vec[1] = rows[16:]
    for copy in copies:
        copy.wait()
    fill_pair(rows, inner_basis, outer_basis, give, keep)
    result.wait()


def last_kernel(recv, coupling, expand, local, second):
    real, imag = field_part(recv, coupling, expand)
    second[0] = local[0] + real
    second[1] = local[1] + imag


ANY = pl.BlockSpec(memory_space=pl.ANY)
RANKS = pl.BlockSpec(memory_space=pltpu.SMEM)
PARAMS = pltpu.CompilerParams(vmem_limit_bytes=16 * 1024 * 1024)


def in_vmem(*arrays):
    return [pltpu.with_memory_space_constraint(a, pltpu.VMEM) for a in arrays]


def in_hbm(*arrays):
    return [pltpu.with_memory_space_constraint(a, pltpu.HBM) for a in arrays]


def call(kernel, outs, *args):
    return pl.pallas_call(
        kernel, in_specs=vmem(len(args)), out_specs=vmem(len(outs)), out_shape=outs, compiler_params=PARAMS
    )(*args)


def exchange(value, groups):
    return lax.all_to_all(value, ALL, split_axis=0, concat_axis=0, axis_index_groups=groups, tiled=True)


def swapped(give, keep, ranks):
    got = lax.ppermute(give, ALL, PARTNER)
    send = pl.pallas_call(
        pair_kernel,
        in_specs=vmem(2) + [RANKS],
        out_specs=vmem(1)[0],
        out_shape=pltpu.VMEM((16, 32, 128), bf16),
        compiler_params=PARAMS,
        name="pair_sums",
    )(*in_vmem(got, keep), ranks)
    return got, send


def crossed(vec):
    return lax.ppermute(vec, ALL, CROSS)


def near_terms(got, vec, near_blocks):
    return pl.pallas_call(
        near_kernel,
        in_specs=vmem(2) + [ANY],
        out_specs=vmem(1)[0],
        out_shape=pltpu.VMEM((2, 16, 512), f32),
        scratch_shapes=[pltpu.VMEM((2, 2, 512, 512), bf16), pltpu.SemaphoreType.DMA((2,))],
        compiler_params=PARAMS,
        name="near_terms",
    )(*in_vmem(got), vec, *in_hbm(near_blocks))


def local_terms(near, cross, recv, near_blocks, coupling, inner_expand):
    other = lax.ppermute(recv, ALL, PARTNER)
    return pl.pallas_call(
        terms_kernel,
        in_specs=vmem(4) + [ANY] * 3,
        out_specs=vmem(1)[0],
        out_shape=pltpu.VMEM((2, 16, 512), f32),
        scratch_shapes=[
            pltpu.VMEM((2, 512, 512), bf16),
            pltpu.VMEM(coupling.shape, bf16),
            pltpu.VMEM(inner_expand.shape, bf16),
            pltpu.SemaphoreType.DMA((3,)),
        ],
        compiler_params=PARAMS,
        name="local_terms",
    )(*in_vmem(near, cross, recv, other), *in_hbm(near_blocks, coupling, inner_expand))


def group_sums(recv):
    send = call(sum_kernel, [pltpu.VMEM((32, 16, 128), bf16)], *in_vmem(recv))[0]
    return exchange(send, PLANE)


def local(probes, near_blocks, inner_basis, coupling, inner_expand, outer_basis, group_coupling, outer_expand, ranks):
    pair = [pltpu.VMEM((160, 128), bf16), pltpu.VMEM((48, 128), f32)]
    give, keep = pl.pallas_call(
        start_kernel,
        in_specs=vmem(3),
        out_specs=vmem(2),
        out_shape=pair,
        compiler_params=PARAMS,
        name="start",
    )(*in_hbm(probes, inner_basis, outer_basis))
    got, send = swapped(give, keep, ranks)
    recv = exchange(send, CHIPS)
    cross = crossed(probes)
    sums = group_sums(recv)
    near = near_terms(got, *in_hbm(probes), near_blocks)
    near = local_terms(near, cross, recv, near_blocks, coupling, inner_expand)
    outs = [jax.ShapeDtypeStruct((2, 16, 512), f32), pltpu.VMEM((2, 16, 512), bf16)] + pair
    weights = in_vmem(group_coupling, outer_expand)
    first, vec, give, keep = pl.pallas_call(
        middle_kernel,
        in_specs=vmem(4) + [ANY] * 2,
        out_specs=[ANY] + vmem(3),
        out_shape=outs,
        scratch_shapes=[
            pltpu.VMEM(inner_basis.shape, bf16),
            pltpu.VMEM(outer_basis.shape, bf16),
            pltpu.VMEM((2, 16, 512), f32),
            pltpu.SemaphoreType.DMA((3,)),
        ],
        compiler_params=PARAMS,
        name="middle",
    )(*in_vmem(sums), *weights, *in_vmem(near), *in_hbm(inner_basis, outer_basis))
    got, send = swapped(give, keep, ranks)
    recv = exchange(send, CHIPS)
    cross = crossed(vec)
    sums = group_sums(recv)
    near = near_terms(got, *in_vmem(vec), near_blocks)
    near = local_terms(near, cross, recv, near_blocks, coupling, inner_expand)
    args = in_vmem(sums) + weights + in_vmem(near)
    second = call(last_kernel, [jax.ShapeDtypeStruct((2, 16, 512), f32)], *args)[0]
    return first, second


def solution(mesh):
    last = P(None, None, ALL)
    placed = (
        last,
        P(None, None, ALL, None),
        last,
        P(None, ALL, None),
        last,
        last,
        P(None, "region", None),
        last,
        P(ALL),
    )
    return jax.shard_map(
        local,
        mesh=mesh,
        in_specs=placed,
        out_specs=(last, last),
        check_vma=False,
    )
```

```python
import jax
import jax.numpy as jnp
from jax import lax
from jax.experimental import pallas as pl
from jax.experimental.pallas import tpu as pltpu
from jax.sharding import PartitionSpec as P

ALL = ("region", "blk")
CHIP_ORDER = tuple(2 * z + y for z in (4, 5, 6, 7, 3, 2, 1, 0) for y in (1, 0))
CHIPS = [[32 * r + 2 * i + c for i in CHIP_ORDER] for r in range(8) for c in range(2)]
PLANE = [[32 * r + 4 * z + q for r in range(8) for q in range(4)] for z in range(8)]
PARTNER = [(d, d ^ 1) for d in range(256)]
CROSS = [(d, d + 1) for d in range(256) if d % 2 == 1 and d % 32 != 31]
CROSS += [(d, d - 1) for d in range(256) if d % 2 == 0 and d % 32 != 0]
NT = (((1,), (1,)), ((), ()))
f32 = jnp.float32
bf16 = jnp.bfloat16


def vmem(n):
    return [pl.BlockSpec(memory_space=pltpu.VMEM)] * n


def nt(rows, mat):
    return lax.dot_general(rows, mat, NT, preferred_element_type=f32)


def nn(rows, mat):
    return jnp.dot(rows, mat, preferred_element_type=f32)


def halves(acc, width):
    real = acc[:16, :width] - acc[16:, width:]
    imag = acc[:16, width:] + acc[16:, :width]
    return real, imag


def paired(acc):
    lane = lax.broadcasted_iota(jnp.int32, (16, 128), 1)
    crossed = pltpu.roll(acc[16:], 64, 1)
    return acc[:16] + jnp.where(lane < 64, -crossed, crossed)


def start_kernel(probes, inner_basis, outer_basis, give, keep, held):
    vec = probes[...].reshape(32, 512)
    held[...] = probes[...]
    real, imag = halves(nt(vec, outer_basis[...].reshape(512, 512)), 256)
    core = lax.rem(lax.axis_index("blk"), 2)
    wide = jnp.concatenate([real, imag], 0)
    low, high = wide[:, :128], wide[:, 128:]
    keep[:16] = paired(nt(vec, inner_basis[...].reshape(128, 512)))
    keep[16:] = jnp.where(core == 0, low, high)
    give[:32] = jnp.where(core == 0, high, low).astype(bf16)
    for k in range(4):
        give[32 + 32 * k : 64 + 32 * k] = vec[:, 128 * k : 128 * k + 128]


def masked(coeff, ranks):
    lane = lax.broadcasted_iota(jnp.int32, (16, 128), 1)
    rank = jnp.where(lane < 64, lane, lane - 64)
    return jnp.where(rank < ranks[0], coeff, 0.0).astype(bf16)


def fill_sends(coeff, quarters, send):
    for d in range(16):
        send[d, :16] = coeff
        send[d, 16:] = quarters[CHIP_ORDER[d] % 2]


def pair_kernel(got, keep, ranks, send):
    quarters = (keep[16:] + got[:32].astype(f32)).astype(bf16)
    fill_sends(masked(keep[:16], ranks), (quarters[:16], quarters[16:]), send)


def sum_kernel(recv, send):
    total = recv[0, 16:].astype(f32)
    for j in range(1, 16):
        total = total + recv[j, 16:].astype(f32)
    total = total.astype(bf16)
    for d in range(32):
        send[d] = total


def near_kernel(got, vec, blocks_hbm, out, blocks, sems):
    other = 2 - 2 * lax.rem(lax.axis_index("blk"), 2)
    copies = [
        pltpu.make_async_copy(blocks_hbm.at[source], blocks.at[slot], sems.at[slot])
        for slot, source in enumerate((1, other))
    ]
    for copy in copies:
        copy.start()
    if got.shape[1] == 128:
        partner = jnp.concatenate([got[32 + 32 * k : 64 + 32 * k] for k in range(4)], 1)
    else:
        partner = got[...]
    copies[0].wait()
    acc = nt(vec[...].reshape(32, 512), blocks[0].reshape(1024, 512))
    copies[1].wait()
    acc = acc + nt(partner, blocks[1].reshape(1024, 512))
    out[0], out[1] = halves(acc, 512)


def terms_kernel(near, cross, recv, other, blocks_hbm, coupling_hbm, expand_hbm, out, block, coupling, expand, sems):
    core = lax.rem(lax.axis_index("blk"), 2)
    copies = [
        pltpu.make_async_copy(coupling_hbm, coupling, sems.at[0]),
        pltpu.make_async_copy(expand_hbm, expand, sems.at[1]),
        pltpu.make_async_copy(blocks_hbm.at[2 * core], block, sems.at[2]),
    ]
    for copy in copies:
        copy.start()
    lane = lax.broadcasted_iota(jnp.int32, (16, 128), 1)
    position = lax.axis_index("blk")
    res, ims = [], []
    for j in range(16):
        mine, theirs = (ref[CHIP_ORDER.index(j), :16].astype(f32) for ref in (recv, other))
        first, second = jnp.where(core == 0, mine, theirs), jnp.where(core == 0, theirs, mine)
        first = jnp.where(jnp.abs(2 * j - position) > 1, first, 0.0)
        second = jnp.where(jnp.abs(2 * j + 1 - position) > 1, second, 0.0)
        res.append(jnp.where(lane < 64, first, pltpu.roll(second, 64, 1)))
        ims.append(jnp.where(lane < 64, pltpu.roll(first, 64, 1), second))
    rows = jnp.concatenate([jnp.concatenate(res, 1), jnp.concatenate(ims, 1)], 0).astype(bf16)
    copies[0].wait()
    inner = paired(nt(rows, coupling[...].reshape(128, 2048)))
    rows = jnp.concatenate([inner[:, :64], pltpu.roll(inner, 64, 1)[:, :64]], 0).astype(bf16)
    copies[1].wait()
    a, b = nn(rows, expand[0]), nn(rows, expand[1])
    copies[2].wait()
    real, imag = halves(nt(cross[...].reshape(32, 512), block[...].reshape(1024, 512)), 512)
    out[0] = near[0] + real + (a[:16] - b[16:])
    out[1] = near[1] + imag + (a[16:] + b[:16])


def field_rows(recv, coupling):
    region = lax.axis_index("region")
    res, ims = [], []
    for s in range(8):
        tiles = [jnp.where(s != region, recv[4 * s + q], jnp.zeros((16, 128), bf16)) for q in range(4)]
        res += tiles[:2]
        ims += tiles[2:]
    rows = jnp.concatenate([jnp.concatenate(res, 1), jnp.concatenate(ims, 1)], 0)
    real, imag = halves(nt(rows, coupling[...].reshape(512, 2048)), 256)
    return jnp.concatenate([real, imag], 0).astype(bf16)


def expanded(rows, expand):
    a, b = nn(rows, expand[0]), nn(rows, expand[1])
    return a[:16] - b[16:], a[16:] + b[:16]


def middle_kernel(recv, coupling, expand, local, mate, ranks, *refs):
    inner_hbm, outer_hbm, mate_outer_hbm, mate_expand_hbm = refs[:4]
    first_hbm, vec, mate_vec, send = refs[4:8]
    inner_basis, outer_basis, mate_expand, first, sems = refs[8:]
    core = lax.rem(lax.axis_index("blk"), 2)
    half = pl.ds(pl.multiple_of(128 * core, 128), 128)
    copies = [
        pltpu.make_async_copy(mate_expand_hbm, mate_expand, sems.at[0]),
        pltpu.make_async_copy(outer_hbm.at[:, half], outer_basis.at[0], sems.at[1]),
        pltpu.make_async_copy(mate_outer_hbm.at[:, half], outer_basis.at[1], sems.at[2]),
        pltpu.make_async_copy(inner_hbm, inner_basis, sems.at[3]),
    ]
    for copy in copies:
        copy.start()
    field = field_rows(recv, coupling)
    real, imag = expanded(field, expand)
    real, imag = local[0] + real, local[1] + imag
    first[0] = real
    first[1] = imag
    result = pltpu.make_async_copy(first, first_hbm, sems.at[4])
    result.start()
    rows = jnp.concatenate([real, imag], 0).astype(bf16)
    vec[0] = rows[:16]
    vec[1] = rows[16:]
    copies[0].wait()
    real, imag = expanded(field, mate_expand)
    mate_rows = jnp.concatenate([mate[0] + real, mate[1] + imag], 0).astype(bf16)
    mate_vec[...] = mate_rows
    for copy in copies[1:]:
        copy.wait()
    wide = nt(rows, outer_basis[0].reshape(256, 512)) + nt(mate_rows, outer_basis[1].reshape(256, 512))
    quarters = [part.astype(bf16) for part in halves(wide, 128)]
    fill_sends(masked(paired(nt(rows, inner_basis[...].reshape(128, 512))), ranks), quarters, send)
    result.wait()


def last_kernel(recv, coupling, expand, local, second):
    real, imag = expanded(field_rows(recv, coupling), expand)
    second[0] = local[0] + real
    second[1] = local[1] + imag


ANY = pl.BlockSpec(memory_space=pl.ANY)
RANKS = pl.BlockSpec(memory_space=pltpu.SMEM)
PARAMS = pltpu.CompilerParams(vmem_limit_bytes=16 * 1024 * 1024)


def in_vmem(*arrays):
    return [pltpu.with_memory_space_constraint(a, pltpu.VMEM) for a in arrays]


def in_hbm(*arrays):
    return [pltpu.with_memory_space_constraint(a, pltpu.HBM) for a in arrays]


def call(kernel, outs, *args):
    return pl.pallas_call(
        kernel, in_specs=vmem(len(args)), out_specs=vmem(len(outs)), out_shape=outs, compiler_params=PARAMS
    )(*args)


def exchange(value, groups):
    return lax.all_to_all(value, ALL, split_axis=0, concat_axis=0, axis_index_groups=groups, tiled=True)


def swapped(give, keep, ranks):
    got = lax.ppermute(give, ALL, PARTNER)
    send = pl.pallas_call(
        pair_kernel,
        in_specs=vmem(2) + [RANKS],
        out_specs=vmem(1)[0],
        out_shape=pltpu.VMEM((16, 32, 128), bf16),
        compiler_params=PARAMS,
        name="pair_sums",
    )(*in_vmem(got, keep), ranks)
    return got, send


def crossed(vec):
    return lax.ppermute(vec, ALL, CROSS)


def near_terms(got, vec, near_blocks):
    return pl.pallas_call(
        near_kernel,
        in_specs=vmem(2) + [ANY],
        out_specs=vmem(1)[0],
        out_shape=pltpu.VMEM((2, 16, 512), f32),
        scratch_shapes=[pltpu.VMEM((2, 2, 512, 512), bf16), pltpu.SemaphoreType.DMA((2,))],
        compiler_params=PARAMS,
        name="near_terms",
    )(*in_vmem(got), vec, *in_hbm(near_blocks))


def local_terms(near, cross, recv, near_blocks, coupling, inner_expand):
    other = lax.ppermute(recv, ALL, PARTNER)
    return pl.pallas_call(
        terms_kernel,
        in_specs=vmem(4) + [ANY] * 3,
        out_specs=vmem(1)[0],
        out_shape=pltpu.VMEM((2, 16, 512), f32),
        scratch_shapes=[
            pltpu.VMEM((2, 512, 512), bf16),
            pltpu.VMEM(coupling.shape, bf16),
            pltpu.VMEM(inner_expand.shape, bf16),
            pltpu.SemaphoreType.DMA((3,)),
        ],
        compiler_params=PARAMS,
        name="local_terms",
    )(*in_vmem(near, cross, recv, other), *in_hbm(near_blocks, coupling, inner_expand))


def group_sums(recv):
    send = call(sum_kernel, [pltpu.VMEM((32, 16, 128), bf16)], *in_vmem(recv))[0]
    return exchange(send, PLANE)


def local(probes, near_blocks, inner_basis, coupling, inner_expand, outer_basis, group_coupling, outer_expand, ranks):
    pair = [pltpu.VMEM((160, 128), bf16), pltpu.VMEM((48, 128), f32), pltpu.VMEM((2, 16, 512), bf16)]
    give, keep, held = pl.pallas_call(
        start_kernel,
        in_specs=vmem(3),
        out_specs=vmem(3),
        out_shape=pair,
        compiler_params=PARAMS,
        name="start",
    )(*in_hbm(probes, inner_basis, outer_basis))
    got, send = swapped(give, keep, ranks)
    recv = exchange(send, CHIPS)
    cross = crossed(probes)
    mate_outer, mate_expand = (lax.ppermute(w, ALL, PARTNER) for w in (outer_basis, outer_expand))
    sums = group_sums(recv)
    near = near_terms(got, *in_vmem(held), near_blocks)
    near = local_terms(near, cross, recv, near_blocks, coupling, inner_expand)
    mate = lax.ppermute(near, ALL, PARTNER)
    weights = in_vmem(group_coupling, outer_expand)
    first, vec, mate_vec, send = pl.pallas_call(
        middle_kernel,
        in_specs=vmem(5) + [RANKS] + [ANY] * 4,
        out_specs=[ANY] + vmem(3),
        out_shape=[
            jax.ShapeDtypeStruct((2, 16, 512), f32),
            pltpu.VMEM((2, 16, 512), bf16),
            pltpu.VMEM((32, 512), bf16),
            pltpu.VMEM((16, 32, 128), bf16),
        ],
        scratch_shapes=[
            pltpu.VMEM(inner_basis.shape, bf16),
            pltpu.VMEM((2, 2, 128, 512), bf16),
            pltpu.VMEM(outer_expand.shape, bf16),
            pltpu.VMEM((2, 16, 512), f32),
            pltpu.SemaphoreType.DMA((5,)),
        ],
        compiler_params=PARAMS,
        name="middle",
    )(*in_vmem(sums), *weights, *in_vmem(near, mate), ranks, *in_hbm(inner_basis, outer_basis, mate_outer, mate_expand))
    recv = exchange(send, CHIPS)
    cross = crossed(vec)
    sums = group_sums(recv)
    near = near_terms(mate_vec, *in_vmem(vec), near_blocks)
    near = local_terms(near, cross, recv, near_blocks, coupling, inner_expand)
    args = in_vmem(sums) + weights + in_vmem(near)
    second = call(last_kernel, [jax.ShapeDtypeStruct((2, 16, 512), f32)], *args)[0]
    return first, second


def solution(mesh):
    last = P(None, None, ALL)
    placed = (
        last,
        P(None, None, ALL, None),
        last,
        P(None, ALL, None),
        last,
        last,
        P(None, "region", None),
        last,
        P(ALL),
    )
    return jax.shard_map(
        local,
        mesh=mesh,
        in_specs=placed,
        out_specs=(last, last),
        check_vma=False,
    )
```

```python
import jax
import jax.numpy as jnp
from jax import lax
from jax.experimental import pallas as pl
from jax.experimental.pallas import tpu as pltpu
from jax.sharding import PartitionSpec as P

ALL = ("region", "blk")
CHIP_ORDER = tuple(2 * z + y for z in (4, 5, 6, 7, 3, 2, 1, 0) for y in (1, 0))
CHIPS = [[32 * r + 2 * i + c for i in CHIP_ORDER] for r in range(8) for c in range(2)]
PLANE_ORDER = tuple(4 * (4 * h + x) + 2 * y + c for x in (2, 3, 1, 0) for h, y in ((1, 0), (1, 1), (0, 1), (0, 0)) for c in (1, 0))
PLANE = [[32 * (k // 4) + 4 * z + k % 4 for k in PLANE_ORDER] for z in range(8)]
PARTNER = [(d, d ^ 1) for d in range(256)]
CROSS = [(d, d + 1) for d in range(256) if d % 2 == 1 and d % 32 != 31]
CROSS += [(d, d - 1) for d in range(256) if d % 2 == 0 and d % 32 != 0]
NT = (((1,), (1,)), ((), ()))
f32 = jnp.float32
bf16 = jnp.bfloat16


def vmem(n):
    return [pl.BlockSpec(memory_space=pltpu.VMEM)] * n


def nt(rows, mat):
    return lax.dot_general(rows, mat, NT, preferred_element_type=f32)


def nn(rows, mat):
    return jnp.dot(rows, mat, preferred_element_type=f32)


def halves(acc, width):
    real = acc[:16, :width] - acc[16:, width:]
    imag = acc[:16, width:] + acc[16:, :width]
    return real, imag


def paired(acc):
    lane = lax.broadcasted_iota(jnp.int32, (16, 128), 1)
    crossed = pltpu.roll(acc[16:], 64, 1)
    return acc[:16] + jnp.where(lane < 64, -crossed, crossed)


def start_kernel(probes, inner_basis, outer_basis, give, keep, held):
    vec = probes[...].reshape(32, 512)
    held[...] = probes[...]
    real, imag = halves(nt(vec, outer_basis[...].reshape(512, 512)), 256)
    core = lax.rem(lax.axis_index("blk"), 2)
    wide = jnp.concatenate([real, imag], 0)
    low, high = wide[:, :128], wide[:, 128:]
    keep[:16] = paired(nt(vec, inner_basis[...].reshape(128, 512)))
    keep[16:] = jnp.where(core == 0, low, high)
    give[:32] = jnp.where(core == 0, high, low).astype(bf16)
    for k in range(4):
        give[32 + 32 * k : 64 + 32 * k] = vec[:, 128 * k : 128 * k + 128]


def masked(coeff, ranks):
    lane = lax.broadcasted_iota(jnp.int32, (16, 128), 1)
    rank = jnp.where(lane < 64, lane, lane - 64)
    return jnp.where(rank < ranks[0], coeff, 0.0).astype(bf16)


def fill_sends(coeff, quarters, send):
    for d in range(16):
        send[d, :16] = coeff
        send[d, 16:] = quarters[CHIP_ORDER[d] % 2]


def pair_kernel(got, keep, ranks, send):
    quarters = (keep[16:] + got[:32].astype(f32)).astype(bf16)
    fill_sends(masked(keep[:16], ranks), (quarters[:16], quarters[16:]), send)


def sum_kernel(recv, send):
    total = recv[0, 16:].astype(f32)
    for j in range(1, 16):
        total = total + recv[j, 16:].astype(f32)
    total = total.astype(bf16)
    for d in range(32):
        send[d] = total


def near_kernel(got, vec, blocks_hbm, out, blocks, sems):
    other = 2 - 2 * lax.rem(lax.axis_index("blk"), 2)
    copies = [
        pltpu.make_async_copy(blocks_hbm.at[source], blocks.at[slot], sems.at[slot])
        for slot, source in enumerate((1, other))
    ]
    for copy in copies:
        copy.start()
    if got.shape[1] == 128:
        partner = jnp.concatenate([got[32 + 32 * k : 64 + 32 * k] for k in range(4)], 1)
    else:
        partner = got[...]
    copies[0].wait()
    acc = nt(vec[...].reshape(32, 512), blocks[0].reshape(1024, 512))
    copies[1].wait()
    acc = acc + nt(partner, blocks[1].reshape(1024, 512))
    out[0], out[1] = halves(acc, 512)


def terms_kernel(near, cross, recv, other, blocks_hbm, coupling_hbm, expand_hbm, out, block, coupling, expand, sems):
    core = lax.rem(lax.axis_index("blk"), 2)
    copies = [
        pltpu.make_async_copy(coupling_hbm, coupling, sems.at[0]),
        pltpu.make_async_copy(expand_hbm, expand, sems.at[1]),
        pltpu.make_async_copy(blocks_hbm.at[2 * core], block, sems.at[2]),
    ]
    for copy in copies:
        copy.start()
    lane = lax.broadcasted_iota(jnp.int32, (16, 128), 1)
    position = lax.axis_index("blk")
    res, ims = [], []
    for j in range(16):
        mine, theirs = (ref[CHIP_ORDER.index(j), :16].astype(f32) for ref in (recv, other))
        first, second = jnp.where(core == 0, mine, theirs), jnp.where(core == 0, theirs, mine)
        first = jnp.where(jnp.abs(2 * j - position) > 1, first, 0.0)
        second = jnp.where(jnp.abs(2 * j + 1 - position) > 1, second, 0.0)
        res.append(jnp.where(lane < 64, first, pltpu.roll(second, 64, 1)))
        ims.append(jnp.where(lane < 64, pltpu.roll(first, 64, 1), second))
    rows = jnp.concatenate([jnp.concatenate(res, 1), jnp.concatenate(ims, 1)], 0).astype(bf16)
    copies[0].wait()
    inner = paired(nt(rows, coupling[...].reshape(128, 2048)))
    rows = jnp.concatenate([inner[:, :64], pltpu.roll(inner, 64, 1)[:, :64]], 0).astype(bf16)
    copies[1].wait()
    a, b = nn(rows, expand[0]), nn(rows, expand[1])
    copies[2].wait()
    real, imag = halves(nt(cross[...].reshape(32, 512), block[...].reshape(1024, 512)), 512)
    out[0] = near[0] + real + (a[:16] - b[16:])
    out[1] = near[1] + imag + (a[16:] + b[:16])


def field_rows(recv, coupling):
    region = lax.axis_index("region")
    res, ims = [], []
    for s in range(8):
        tiles = [jnp.where(s != region, recv[PLANE_ORDER.index(4 * s + q)], jnp.zeros((16, 128), bf16)) for q in range(4)]
        res += tiles[:2]
        ims += tiles[2:]
    rows = jnp.concatenate([jnp.concatenate(res, 1), jnp.concatenate(ims, 1)], 0)
    real, imag = halves(nt(rows, coupling[...].reshape(512, 2048)), 256)
    return jnp.concatenate([real, imag], 0).astype(bf16)


def expanded(rows, expand):
    a, b = nn(rows, expand[0]), nn(rows, expand[1])
    return a[:16] - b[16:], a[16:] + b[:16]


def middle_kernel(recv, coupling, expand, local, mate, ranks, *refs):
    inner_hbm, outer_hbm, mate_outer_hbm, mate_expand_hbm = refs[:4]
    first_hbm, vec, mate_vec, send = refs[4:8]
    inner_basis, outer_basis, mate_expand, first, sems = refs[8:]
    core = lax.rem(lax.axis_index("blk"), 2)
    half = pl.ds(pl.multiple_of(128 * core, 128), 128)
    copies = [
        pltpu.make_async_copy(mate_expand_hbm, mate_expand, sems.at[0]),
        pltpu.make_async_copy(outer_hbm.at[:, half], outer_basis.at[0], sems.at[1]),
        pltpu.make_async_copy(mate_outer_hbm.at[:, half], outer_basis.at[1], sems.at[2]),
        pltpu.make_async_copy(inner_hbm, inner_basis, sems.at[3]),
    ]
    for copy in copies:
        copy.start()
    field = field_rows(recv, coupling)
    real, imag = expanded(field, expand)
    real, imag = local[0] + real, local[1] + imag
    first[0] = real
    first[1] = imag
    result = pltpu.make_async_copy(first, first_hbm, sems.at[4])
    result.start()
    rows = jnp.concatenate([real, imag], 0).astype(bf16)
    vec[0] = rows[:16]
    vec[1] = rows[16:]
    copies[0].wait()
    real, imag = expanded(field, mate_expand)
    mate_rows = jnp.concatenate([mate[0] + real, mate[1] + imag], 0).astype(bf16)
    mate_vec[...] = mate_rows
    for copy in copies[1:]:
        copy.wait()
    wide = nt(rows, outer_basis[0].reshape(256, 512)) + nt(mate_rows, outer_basis[1].reshape(256, 512))
    quarters = [part.astype(bf16) for part in halves(wide, 128)]
    fill_sends(masked(paired(nt(rows, inner_basis[...].reshape(128, 512))), ranks), quarters, send)
    result.wait()


def last_kernel(recv, coupling, expand, local, second):
    real, imag = expanded(field_rows(recv, coupling), expand)
    second[0] = local[0] + real
    second[1] = local[1] + imag


ANY = pl.BlockSpec(memory_space=pl.ANY)
RANKS = pl.BlockSpec(memory_space=pltpu.SMEM)
PARAMS = pltpu.CompilerParams(vmem_limit_bytes=16 * 1024 * 1024)


def in_vmem(*arrays):
    return [pltpu.with_memory_space_constraint(a, pltpu.VMEM) for a in arrays]


def in_hbm(*arrays):
    return [pltpu.with_memory_space_constraint(a, pltpu.HBM) for a in arrays]


def call(kernel, outs, *args):
    return pl.pallas_call(
        kernel, in_specs=vmem(len(args)), out_specs=vmem(len(outs)), out_shape=outs, compiler_params=PARAMS
    )(*args)


def exchange(value, groups):
    return lax.all_to_all(value, ALL, split_axis=0, concat_axis=0, axis_index_groups=groups, tiled=True)


def swapped(give, keep, ranks):
    got = lax.ppermute(give, ALL, PARTNER)
    send = pl.pallas_call(
        pair_kernel,
        in_specs=vmem(2) + [RANKS],
        out_specs=vmem(1)[0],
        out_shape=pltpu.VMEM((16, 32, 128), bf16),
        compiler_params=PARAMS,
        name="pair_sums",
    )(*in_vmem(got, keep), ranks)
    return got, send


def crossed(vec):
    return lax.ppermute(vec, ALL, CROSS)


def near_terms(got, vec, near_blocks):
    return pl.pallas_call(
        near_kernel,
        in_specs=vmem(2) + [ANY],
        out_specs=vmem(1)[0],
        out_shape=pltpu.VMEM((2, 16, 512), f32),
        scratch_shapes=[pltpu.VMEM((2, 2, 512, 512), bf16), pltpu.SemaphoreType.DMA((2,))],
        compiler_params=PARAMS,
        name="near_terms",
    )(*in_vmem(got), vec, *in_hbm(near_blocks))


def local_terms(near, cross, recv, near_blocks, coupling, inner_expand):
    other = lax.ppermute(recv, ALL, PARTNER)
    return pl.pallas_call(
        terms_kernel,
        in_specs=vmem(4) + [ANY] * 3,
        out_specs=vmem(1)[0],
        out_shape=pltpu.VMEM((2, 16, 512), f32),
        scratch_shapes=[
            pltpu.VMEM((2, 512, 512), bf16),
            pltpu.VMEM(coupling.shape, bf16),
            pltpu.VMEM(inner_expand.shape, bf16),
            pltpu.SemaphoreType.DMA((3,)),
        ],
        compiler_params=PARAMS,
        name="local_terms",
    )(*in_vmem(near, cross, recv, other), *in_hbm(near_blocks, coupling, inner_expand))


def group_sums(recv):
    send = call(sum_kernel, [pltpu.VMEM((32, 16, 128), bf16)], *in_vmem(recv))[0]
    return exchange(send, PLANE)


def local(probes, near_blocks, inner_basis, coupling, inner_expand, outer_basis, group_coupling, outer_expand, ranks):
    pair = [pltpu.VMEM((160, 128), bf16), pltpu.VMEM((48, 128), f32), pltpu.VMEM((2, 16, 512), bf16)]
    give, keep, held = pl.pallas_call(
        start_kernel,
        in_specs=vmem(3),
        out_specs=vmem(3),
        out_shape=pair,
        compiler_params=PARAMS,
        name="start",
    )(*in_hbm(probes, inner_basis, outer_basis))
    got, send = swapped(give, keep, ranks)
    recv = exchange(send, CHIPS)
    cross = crossed(probes)
    mate_outer, mate_expand = (lax.ppermute(w, ALL, PARTNER) for w in (outer_basis, outer_expand))
    sums = group_sums(recv)
    near = near_terms(got, *in_vmem(held), near_blocks)
    near = local_terms(near, cross, recv, near_blocks, coupling, inner_expand)
    mate = lax.ppermute(near, ALL, PARTNER)
    weights = in_vmem(group_coupling, outer_expand)
    first, vec, mate_vec, send = pl.pallas_call(
        middle_kernel,
        in_specs=vmem(5) + [RANKS] + [ANY] * 4,
        out_specs=[ANY] + vmem(3),
        out_shape=[
            jax.ShapeDtypeStruct((2, 16, 512), f32),
            pltpu.VMEM((2, 16, 512), bf16),
            pltpu.VMEM((32, 512), bf16),
            pltpu.VMEM((16, 32, 128), bf16),
        ],
        scratch_shapes=[
            pltpu.VMEM(inner_basis.shape, bf16),
            pltpu.VMEM((2, 2, 128, 512), bf16),
            pltpu.VMEM(outer_expand.shape, bf16),
            pltpu.VMEM((2, 16, 512), f32),
            pltpu.SemaphoreType.DMA((5,)),
        ],
        compiler_params=PARAMS,
        name="middle",
    )(*in_vmem(sums), *weights, *in_vmem(near, mate), ranks, *in_hbm(inner_basis, outer_basis, mate_outer, mate_expand))
    recv = exchange(send, CHIPS)
    cross = crossed(vec)
    sums = group_sums(recv)
    near = near_terms(mate_vec, *in_vmem(vec), near_blocks)
    near = local_terms(near, cross, recv, near_blocks, coupling, inner_expand)
    args = in_vmem(sums) + weights + in_vmem(near)
    second = call(last_kernel, [jax.ShapeDtypeStruct((2, 16, 512), f32)], *args)[0]
    return first, second


def solution(mesh):
    last = P(None, None, ALL)
    placed = (
        last,
        P(None, None, ALL, None),
        last,
        P(None, ALL, None),
        last,
        last,
        P(None, "region", None),
        last,
        P(ALL),
    )
    return jax.shard_map(
        local,
        mesh=mesh,
        in_specs=placed,
        out_specs=(last, last),
        check_vma=False,
    )
```
